32 devices in a mesh: dp: 4 (over y, x), mp: 8 (over z, core).
Axes of the slice: x: 2, y: 2, z: 4, core: 2. Of those that a mesh axis runs over, the one named last changes fastest.
Arguments:
- grads: bfloat16 [3, 8192, 28672], P(None, 'dp', 'mp'), may hold values from -8 to 8
- sketch: bfloat16 [28672, 256], P('mp'), may hold values from -0.03125 to 0.03125
- old_proj: bfloat16 [3, 8192, 256], P(None, 'dp'), may hold values from -0.0625 to 0.0625
- first_moment: float32 [3, 256, 28672], P(None, 'dp', 'mp'), may hold values from -12 to 12
- second_moment: float32 [3, 256, 28672], P(None, 'dp', 'mp'), may hold values from 0.25 to 4
- refresh_list: int32 [1], replicated, may hold values from 0 to 2
Outputs:
- new_first: float32 [3, 256, 28672], P(None, 'dp', 'mp')
- new_second: float32 [3, 256, 28672], P(None, 'dp', 'mp')
- direction: bfloat16 [3, 256, 28672], P(None, 'dp', 'mp')
The draws below stay inside these ranges and needn't reach their ends.
All inputs are finite; a program needn't handle non-finite values.
Results may differ from the reference program's by a relative error of at most 0.0029.
Values sent between devices are 32-bit elements; how exact they have to be, the bound alone decides.
No kernel may reach another device: no remote copies, remote signals or barrier semaphores. Data moves between devices by JAX's collectives and lax.ppermute only.
A program may use at most 192 MiB of HBM per device.

```python
import math
import jax
import jax.numpy as jnp
from jax import lax

D = 8192
FF = 28672
RANK = 256
MATS = 3


def draw_grads(key, part):
    base_key = jax.random.fold_in(key, 11)
    values = jnp.clip(jax.random.normal(base_key, (MATS, D, FF), jnp.float32), -6.0, 6.0)
    return values.astype(jnp.bfloat16)


def block_scale(own_key, dims, cuts, least, top_value):
    loudness, own = 1.0, jax.random.fold_in(own_key, 6)
    for position, shards_of in cuts:
        heights = jnp.exp(jax.random.uniform(jax.random.fold_in(own, position), (shards_of,), jnp.float32, least / len(cuts), top_value / len(cuts)))
        loudness = loudness * jnp.repeat(heights, dims[position] // shards_of).reshape([-1 if axis == position else 1 for axis in range(len(dims))])
    return loudness


def scatter_about(key, extent, scale, reach, pieces=(), held_as=jnp.bfloat16):
    level = block_scale(key, extent, pieces, -0.22, 0.18) if pieces else 1.0
    values = jax.random.normal(key, extent, jnp.float32) * scale * level
    return jnp.minimum(jnp.maximum(values, -reach), reach).astype(held_as)


def setup_inputs(seed: int = 0) -> dict:
    keys = jax.random.split(jax.random.key(seed), 7)
    grads = draw_grads(jax.random.fold_in(keys[6], 71), 0)
    sketch = scatter_about(keys[1], (FF, RANK), FF ** -0.5, 0.03125, ((0, 8),))
    old_proj = scatter_about(keys[2], (MATS, D, RANK), D ** -0.5, 0.0625, ((1, 4),))
    first_moment = scatter_about(keys[3], (MATS, RANK, FF), 2.0, 12.0, ((1, 4), (2, 8)), jnp.float32)
    second_moment = jnp.clip(jnp.exp(math.log(4.0) - 2.7725887 * jax.random.uniform(keys[4], (MATS, RANK, FF), jnp.float32) ** block_scale(keys[4], (MATS, RANK, FF), ((1, 4), (2, 8)), -0.2, 0.2)), 0.25, 4.0)
    refresh_list = jax.random.randint(keys[5], (1,), 0, MATS).astype(jnp.int32)
    return dict(grads=grads, sketch=sketch, old_proj=old_proj, first_moment=first_moment, second_moment=second_moment, refresh_list=refresh_list)


first_decay = 0.9
second_decay = 0.95
epsilon = 1e-08
highest = lax.Precision.HIGHEST

def reference(grads, sketch, old_proj, first_moment, second_moment, refresh_list):
    chosen = refresh_list[0]
    target = lax.dynamic_index_in_dim(grads, chosen, 0, keepdims=False)
    prior_proj = lax.dynamic_index_in_dim(old_proj, chosen, 0, keepdims=False).astype(jnp.float32)
    sketched = (jnp.dot(target.astype(jnp.float32), sketch.astype(jnp.float32), preferred_element_type=jnp.float32) / RANK).astype(jnp.bfloat16)
    backward = (jnp.dot(target.T.astype(jnp.float32), sketched.astype(jnp.float32), preferred_element_type=jnp.float32) / FF).astype(jnp.bfloat16)
    range_panel = jnp.dot(target.astype(jnp.float32), backward.astype(jnp.float32), preferred_element_type=jnp.float32)
    gram_full = jnp.dot(range_panel.T, range_panel, precision=highest)
    factor = jnp.linalg.cholesky(gram_full)
    new_basis = jax.scipy.linalg.solve_triangular(factor, range_panel.T, lower=True).T
    turning = jnp.dot(new_basis.T, prior_proj, precision=highest)
    new_proj = new_basis.astype(jnp.bfloat16)
    first_list = []
    second_list = []
    direction_list = []
    for matrix in range(MATS):
        fresh = chosen == matrix
        projector = jnp.where(fresh, new_proj, old_proj[matrix])
        projected = jnp.dot(projector.T.astype(jnp.float32), grads[matrix].astype(jnp.float32), preferred_element_type=jnp.float32)
        turned_first = jnp.where(fresh, jnp.dot(turning, first_moment[matrix], precision=highest), first_moment[matrix])
        turned_second = jnp.where(fresh, jnp.dot(turning * turning, second_moment[matrix], precision=highest), second_moment[matrix])
        updated_first = first_decay * turned_first + (1.0 - first_decay) * projected
        updated_second = second_decay * turned_second + (1.0 - second_decay) * projected * projected
        first_list.append(updated_first)
        second_list.append(updated_second)
        direction_list.append((updated_first / (jnp.sqrt(updated_second) + epsilon)).astype(jnp.bfloat16))
    return (jnp.stack(first_list), jnp.stack(second_list), jnp.stack(direction_list))
```

```python
import jax
import jax.numpy as jnp
from jax import lax
from jax.sharding import PartitionSpec as P

first_decay = 0.9
second_decay = 0.95
epsilon = 1e-08
highest = lax.Precision.HIGHEST


def bits_of(axis_name):
    return (lax.axis_size(axis_name) - 1).bit_length()


def flip(value, axis_name, bit):
    size = lax.axis_size(axis_name)
    return lax.ppermute(value, axis_name, [(i, i ^ (1 << bit)) for i in range(size)])


def own_bit(axis_name, bit):
    return (lax.axis_index(axis_name) >> bit) & 1


def orders(axis_name):
    bits = list(range(bits_of(axis_name)))
    if axis_name == "mp":
        return bits, bits[:1] + bits[:0:-1]
    return bits, bits[::-1]


def dims_of(order, bit, done):
    return sum(1 for other in order[done:] if other > bit)


def halving(block, axis_name, order):
    count = len(order)
    size = 1 << count
    rows, columns = block.shape[0] // size, block.shape[1]
    value = block.reshape((2,) * count + (rows, columns))
    for done, bit in enumerate(order):
        place = dims_of(order, bit, done)
        mine = own_bit(axis_name, bit)
        keep = lax.dynamic_index_in_dim(value, mine, place, keepdims=False)
        send = lax.dynamic_index_in_dim(value, 1 - mine, place, keepdims=False)
        value = keep + flip(send, axis_name, bit)
    return value


def doubling(block, axis_name, order):
    rows, columns = block.shape
    count = len(order)
    value = block
    for done in range(count - 1, -1, -1):
        bit = order[done]
        place = dims_of(order, bit, done)
        mine = own_bit(axis_name, bit)
        other = flip(value, axis_name, bit)
        low = jnp.where(mine == 0, value, other)
        high = jnp.where(mine == 0, other, value)
        value = jnp.stack([low, high], axis=place)
    return value.reshape((1 << count) * rows, columns)


def halves(block):
    middle = block.shape[-1] // 2
    return block[..., :middle], block[..., middle:]


def scatter_sum(block, axis_name):
    return [
        halving(half, axis_name, order) for half, order in zip(halves(block), orders(axis_name))
    ]


def gather_rows(pieces, axis_name):
    return [doubling(piece, axis_name, order) for piece, order in zip(pieces, orders(axis_name))]


def full_sum(block, axis_name):
    return gather_rows(scatter_sum(block, axis_name), axis_name)


def small_sum(block, axis_name):
    pieces = []
    for half, order in zip(halves(block), orders(axis_name)):
        for bit in order:
            half = half + flip(half, axis_name, bit)
        pieces.append(half)
    return jnp.concatenate(pieces, axis=-1)


def product(left, right):
    return jnp.dot(left, right, precision=highest, preferred_element_type=jnp.float32)


def columns_product(left, right, **options):
    return lax.dot_general(
        left, right, (((0,), (0,)), ((), ())), preferred_element_type=jnp.float32, **options
    )


def inverse_factor(gram):
    half = gram.shape[0] // 2
    eye = jnp.eye(half, dtype=jnp.float32)
    top = jnp.linalg.cholesky(gram[:half, :half])
    top_inverse = jax.scipy.linalg.solve_triangular(top, eye, lower=True)
    side = product(gram[half:, :half], top_inverse.T)
    low = jnp.linalg.cholesky(gram[half:, half:] - product(side, side.T))
    low_inverse = jax.scipy.linalg.solve_triangular(low, eye, lower=True)
    corner = -product(low_inverse, product(side, top_inverse))
    return jnp.concatenate(
        [
            jnp.concatenate([top_inverse, jnp.zeros_like(eye)], axis=1),
            jnp.concatenate([corner, low_inverse], axis=1),
        ],
        axis=0,
    )


def updates(moved_first, moved_second, projected):
    first = first_decay * moved_first + (1.0 - first_decay) * projected
    second = second_decay * moved_second + (1.0 - second_decay) * projected * projected
    return first, second, (first / (jnp.sqrt(second) + epsilon)).astype(jnp.bfloat16)


def local(grads, sketch, old_proj, first_moment, second_moment, refresh_list):
    chosen = refresh_list[0]
    matrix_count = grads.shape[0]
    rank_rows = first_moment.shape[1]
    rank_total = sketch.shape[1]
    columns_total = sketch.shape[0] * lax.axis_size("mp")

    def pick(array, index):
        return lax.dynamic_index_in_dim(array, index, 0, keepdims=False)

    target = pick(grads, chosen)
    prior_proj = pick(old_proj, chosen).astype(jnp.float32)
    first_all = lax.all_gather(pick(first_moment, chosen), "dp", axis=0, tiled=True)
    second_all = lax.all_gather(pick(second_moment, chosen), "dp", axis=0, tiled=True)
    others = [lax.rem(chosen + step, matrix_count) for step in range(1, matrix_count)]

    sketch_part = jnp.dot(target, sketch, preferred_element_type=jnp.float32)
    sketched = jnp.concatenate(
        [(half / rank_total).astype(jnp.bfloat16) for half in full_sum(sketch_part, "mp")], axis=1
    )
    other_parts = jnp.stack(
        [columns_product(pick(old_proj, k), pick(grads, k)) for k in others], axis=1
    )
    backward_part = columns_product(target, sketched)
    backward_part, other_parts = lax.optimization_barrier((backward_part, other_parts))
    backward = jnp.concatenate(
        [
            (half / columns_total).astype(jnp.bfloat16)
            for half in full_sum(backward_part, "dp")
        ],
        axis=1,
    )
    backward, other_parts = lax.optimization_barrier((backward, other_parts))
    other_projected = lax.psum_scatter(other_parts, "dp", scatter_dimension=0, tiled=True)
    range_panel = jnp.concatenate(
        full_sum(jnp.dot(target, backward, preferred_element_type=jnp.float32), "mp"), axis=1
    )
    even = own_bit("mp", 0) == 0
    paired = small_sum(
        columns_product(range_panel, jnp.where(even, range_panel, prior_proj), precision=highest),
        "dp",
    )
    swapped = flip(paired, "mp", 0)
    gram = jnp.where(even, paired, swapped)
    overlap = jnp.where(even, swapped, paired)
    inverse = inverse_factor(gram)
    new_basis = lax.dot_general(
        range_panel,
        inverse,
        (((1,), (1,)), ((), ())),
        precision=highest,
        preferred_element_type=jnp.float32,
    ).astype(jnp.bfloat16)
    own_projected = jnp.concatenate(
        scatter_sum(columns_product(new_basis, target), "dp"), axis=1
    )
    own_start = lax.axis_index("dp") * rank_rows
    own_turning = product(lax.dynamic_slice_in_dim(inverse, own_start, rank_rows, 0), overlap)
    turned_first = product(own_turning, first_all)
    turned_second = product(own_turning * own_turning, second_all)

    results = [
        updates(pick(first_moment, k), pick(second_moment, k), other_projected[:, place])
        for place, k in enumerate(others)
    ]
    results.append(updates(turned_first, turned_second, own_projected))
    shape = first_moment.shape
    outs = [
        first_moment,
        second_moment,
        jnp.zeros(shape, jnp.bfloat16),
    ]
    for k, result in zip(others + [chosen], results):
        outs = [lax.dynamic_update_index_in_dim(o, r, k, 0) for o, r in zip(outs, result)]
    return tuple(outs)


def solution(mesh):
    placed = (
        P(None, "dp", "mp"),
        P("mp", None),
        P(None, "dp", None),
        P(None, "dp", "mp"),
        P(None, "dp", "mp"),
        P(),
    )
    return jax.shard_map(
        local,
        mesh=mesh,
        in_specs=placed,
        out_specs=(P(None, "dp", "mp"), P(None, "dp", "mp"), P(None, "dp", "mp")),
        check_vma=False,
    )
```

```python
import jax
import jax.numpy as jnp
from jax import lax
from jax.sharding import PartitionSpec as P


first_decay = 0.9
second_decay = 0.95
epsilon = 1e-08
highest = lax.Precision.HIGHEST


def bits_of(axis_name):
    return (lax.axis_size(axis_name) - 1).bit_length()


def flip(value, axis_name, bit):
    size = lax.axis_size(axis_name)
    return lax.ppermute(value, axis_name, [(i, i ^ (1 << bit)) for i in range(size)])


def own_bit(axis_name, bit):
    return (lax.axis_index(axis_name) >> bit) & 1


def orders(axis_name):
    bits = list(range(bits_of(axis_name)))
    if axis_name == "mp":
        return bits, bits[:1] + bits[:0:-1]
    return bits, bits[::-1]


def dims_of(order, bit, done):
    return sum(1 for other in order[done:] if other > bit)


def halving(block, axis_name, order):
    count = len(order)
    size = 1 << count
    rows, columns = block.shape[0] // size, block.shape[1]
    value = block.reshape((2,) * count + (rows, columns))
    for done, bit in enumerate(order):
        place = dims_of(order, bit, done)
        mine = own_bit(axis_name, bit)
        keep = lax.dynamic_index_in_dim(value, mine, place, keepdims=False)
        send = lax.dynamic_index_in_dim(value, 1 - mine, place, keepdims=False)
        value = keep + flip(send, axis_name, bit)
    return value


def doubling(block, axis_name, order):
    rows, columns = block.shape
    count = len(order)
    value = block
    for done in range(count - 1, -1, -1):
        bit = order[done]
        place = dims_of(order, bit, done)
        mine = own_bit(axis_name, bit)
        other = flip(value, axis_name, bit)
        low = jnp.where(mine == 0, value, other)
        high = jnp.where(mine == 0, other, value)
        value = jnp.stack([low, high], axis=place)
    return value.reshape((1 << count) * rows, columns)


def halves(block):
    middle = block.shape[-1] // 2
    return block[..., :middle], block[..., middle:]


def scatter_sum(block, axis_name):
    return [
        halving(half, axis_name, order) for half, order in zip(halves(block), orders(axis_name))
    ]


def gather_rows(pieces, axis_name):
    return [doubling(piece, axis_name, order) for piece, order in zip(pieces, orders(axis_name))]


def full_sum(block, axis_name):
    return gather_rows(scatter_sum(block, axis_name), axis_name)


def small_sum(block, axis_name):
    pieces = []
    for half, order in zip(halves(block), orders(axis_name)):
        for bit in order:
            half = half + flip(half, axis_name, bit)
        pieces.append(half)
    return jnp.concatenate(pieces, axis=-1)


def product(left, right):
    return jnp.dot(left, right, precision=highest, preferred_element_type=jnp.float32)


def columns_product(left, right, **options):
    return lax.dot_general(
        left, right, (((0,), (0,)), ((), ())), preferred_element_type=jnp.float32, **options
    )


def inverse_factor(gram):
    half = gram.shape[0] // 2
    eye = jnp.eye(half, dtype=jnp.float32)
    top = jnp.linalg.cholesky(gram[:half, :half])
    top_inverse = jax.scipy.linalg.solve_triangular(top, eye, lower=True)
    side = product(gram[half:, :half], top_inverse.T)
    low = jnp.linalg.cholesky(gram[half:, half:] - product(side, side.T))
    low_inverse = jax.scipy.linalg.solve_triangular(low, eye, lower=True)
    corner = -product(low_inverse, product(side, top_inverse))
    return jnp.concatenate(
        [
            jnp.concatenate([top_inverse, jnp.zeros_like(eye)], axis=1),
            jnp.concatenate([corner, low_inverse], axis=1),
        ],
        axis=0,
    )


def updates(moved_first, moved_second, projected):
    first = first_decay * moved_first + (1.0 - first_decay) * projected
    second = second_decay * moved_second + (1.0 - second_decay) * projected * projected
    return first, second, (first / (jnp.sqrt(second) + epsilon)).astype(jnp.bfloat16)


def step(grads, sketch, old_proj, first_moment, second_moment, refresh_list):
    chosen = refresh_list[0]
    matrix_count = grads.shape[0]
    rank_rows = first_moment.shape[1]
    rank_total = sketch.shape[1]
    columns_total = sketch.shape[0] * lax.axis_size("mp")

    def pick(array, index):
        return lax.dynamic_index_in_dim(array, index, 0, keepdims=False)

    target = pick(grads, chosen)
    prior_proj = pick(old_proj, chosen).astype(jnp.float32)
    first_own, second_own = lax.optimization_barrier(
        (pick(first_moment, chosen), pick(second_moment, chosen))
    )
    first_all = lax.all_gather(first_own, "dp", axis=0, tiled=True)
    second_all = lax.all_gather(second_own, "dp", axis=0, tiled=True)
    others = [lax.rem(chosen + step, matrix_count) for step in range(1, matrix_count)]

    sketch_part = jnp.dot(target, sketch, preferred_element_type=jnp.float32)
    sketched = jnp.concatenate(
        [(half / rank_total).astype(jnp.bfloat16) for half in full_sum(sketch_part, "mp")], axis=1
    )
    other_parts = jnp.stack(
        [columns_product(pick(old_proj, k), pick(grads, k)) for k in others], axis=1
    )
    backward_part = columns_product(target, sketched)
    backward_part, other_parts = lax.optimization_barrier((backward_part, other_parts))
    backward = jnp.concatenate(
        [
            (half / columns_total).astype(jnp.bfloat16)
            for half in full_sum(backward_part, "dp")
        ],
        axis=1,
    )
    backward, other_parts = lax.optimization_barrier((backward, other_parts))
    other_projected = lax.psum_scatter(other_parts, "dp", scatter_dimension=0, tiled=True)
    range_part = jnp.dot(target, backward, preferred_element_type=jnp.float32)
    range_panel = jnp.concatenate(full_sum(range_part, "mp"), axis=1)
    even = own_bit("mp", 0) == 0
    paired = small_sum(
        columns_product(range_panel, jnp.where(even, range_panel, prior_proj), precision=highest),
        "dp",
    )
    swapped = flip(paired, "mp", 0)
    gram = jnp.where(even, paired, swapped)
    overlap = jnp.where(even, swapped, paired)
    inverse = inverse_factor(gram)
    new_basis = lax.dot_general(
        range_panel,
        inverse,
        (((1,), (1,)), ((), ())),
        precision=highest,
        preferred_element_type=jnp.float32,
    ).astype(jnp.bfloat16)
    projected_part = columns_product(new_basis, target)
    projected_part, other_projected, late_first, late_second = lax.optimization_barrier(
        (projected_part, other_projected, first_moment, second_moment)
    )
    own_projected = jnp.concatenate(scatter_sum(projected_part, "dp"), axis=1)
    own_start = lax.axis_index("dp") * rank_rows
    own_turning = product(lax.dynamic_slice_in_dim(inverse, own_start, rank_rows, 0), overlap)
    turned_first = product(own_turning, first_all)
    turned_second = product(own_turning * own_turning, second_all)

    results = [
        updates(pick(late_first, k), pick(late_second, k), other_projected[:, place])
        for place, k in enumerate(others)
    ]
    results.append(updates(turned_first, turned_second, own_projected))
    shape = first_moment.shape
    outs = [
        late_first,
        late_second,
        jnp.zeros(shape, jnp.bfloat16),
    ]
    for k, result in zip(others + [chosen], results):
        outs = [lax.dynamic_update_index_in_dim(o, r, k, 0) for o, r in zip(outs, result)]
    return tuple(outs)


def solution(mesh):
    placed = (
        P(None, "dp", "mp"),
        P("mp", None),
        P(None, "dp", None),
        P(None, "dp", "mp"),
        P(None, "dp", "mp"),
        P(),
    )
    return jax.shard_map(
        step,
        mesh=mesh,
        in_specs=placed,
        out_specs=(P(None, "dp", "mp"), P(None, "dp", "mp"), P(None, "dp", "mp")),
        check_vma=False,
    )
```
